512 devices in a mesh: range: 32 (over x, z_hi, y), ping: 16 (over z_lo, core).
Axes of the slice: x: 4, y: 4, z: 16 (z_hi: 2, z_lo: 8; z = z_hi * 8 + z_lo), core: 2. Of those that a mesh axis runs over, the one named last changes fastest.
Arguments:
- echoes: bfloat16 [128, 32, 4096], P('ping', None, 'range'), may hold values from -6 to 6
- band_offset: int32 [128], P('ping'), may hold values from -128 to 64
- sway_delay: float32 [128, 32], P('ping'), may hold values from 0 to 1
- channel_gain: float32 [128, 32], P('ping'), may hold values from 0.5 to 2
- track_bin: int32 [128], P('ping'), may hold values from 0 to 2047
Outputs:
- image_real: float32 [2048, 4096], P('ping', 'range')
- image_imag: float32 [2048, 4096], P('ping', 'range')
The draws below stay inside these ranges and needn't reach their ends.
All inputs are finite; a program needn't handle non-finite values.
Results may differ from the reference program's by a relative error of at most 0.017.
Values may be sent and summed in bfloat16 or wider, within the bound.
A program may use at most 64 MiB of HBM per device.

```python
import math
import jax
import jax.numpy as jnp
from jax import lax

C = 32
X = 2048
BAND = 64
HALO = 128
PING_DEV = 8
R_DEV = 128
PINGS = 128
RANGE = 4096
N_PING = 16


def place_ends(entries, key, smallest, largest):
    index_at = [jax.random.randint(jax.random.fold_in(key, axis), (), 0, length) for axis, length in enumerate(entries.shape)]
    longest = entries.shape.index(max(entries.shape))
    next_to = index_at[:longest] + [(index_at[longest] + 1) % entries.shape[longest]] + index_at[longest + 1:]
    return entries.at[tuple(index_at)].set(smallest).at[tuple(next_to)].set(largest)


def levels(stream_key, extent, cuts, least, largest):
    def one(axis_at, blocks):
        draws = jax.random.uniform(jax.random.fold_in(jax.random.fold_in(stream_key, 6), axis_at), (blocks,), jnp.float32, least / len(cuts), largest / len(cuts))
        return jnp.repeat(jnp.exp(draws), extent[axis_at] // blocks).reshape((-1,) + (1,) * (len(extent) - axis_at - 1))

    gain = one(*cuts[0])
    for cut in cuts[1:]:
        gain = gain * one(*cut)
    return gain


def normal_values(stream_key, dims, scale, limit, cuts=(), kind=jnp.bfloat16):
    values = scale * jax.random.normal(stream_key, dims, jnp.float32)
    if cuts:
        values = values * levels(stream_key, dims, cuts, -0.22, 0.18)
    return jnp.clip(values, -limit, limit).astype(kind)


def setup_inputs(seed: int = 0) -> dict:
    streams_of = jax.random.split(jax.random.key(seed), 6)
    return {
        "echoes": normal_values(streams_of[0], (PINGS, C, RANGE), 1.0, 6.0, ((0, 16), (2, 32))),
        "band_offset": place_ends(jax.random.randint(streams_of[1], (PINGS,), -HALO, HALO - BAND + 1), jax.random.fold_in(streams_of[1], 1), -HALO, HALO - BAND).astype(jnp.int32),
        "sway_delay": jnp.clip(1.0 * jax.random.uniform(streams_of[2], (PINGS, C), jnp.float32) ** levels(streams_of[2], (PINGS, C), ((0, 16),), -0.2, 0.2), 0.0, 1.0),
        "channel_gain": jnp.clip(jnp.exp(math.log(2.0) - 1.3862944 * jax.random.uniform(streams_of[3], (PINGS, C), jnp.float32) ** levels(streams_of[3], (PINGS, C), ((0, 16),), -0.2, 0.2)), 0.5, 2.0),
        "track_bin": place_ends(jax.random.randint(streams_of[4], (PINGS,), 0, X), jax.random.fold_in(streams_of[4], 1), 0, X - 1).astype(jnp.int32),
    }


def make_taps(sway_delay, channel_gain):
    kpos = jnp.arange(BAND, dtype=jnp.float32)
    shift = kpos - (BAND / 2 - 1) - sway_delay[..., None]
    window = 0.5 - 0.5 * jnp.cos(2.0 * math.pi * (kpos + 0.5) / BAND)
    return jnp.sinc(shift) * window * channel_gain[..., None]

def compensate(padded, offsets, taps, samples):
    padded = padded.astype(jnp.float32)
    ping_count, channels, _ = padded.shape

    def pick(row, shift):
        return lax.dynamic_slice_in_dim(row, (shift + HALO).astype(jnp.int32), samples + BAND - 1, 1)
    windows = jax.vmap(pick)(padded, offsets)
    lhs = windows.reshape(1, ping_count * channels, samples + BAND - 1)
    rhs = taps.reshape(ping_count * channels, 1, BAND).astype(jnp.float32)
    result = lax.conv_general_dilated(lhs, rhs, (1,), 'VALID', dimension_numbers=('NCH', 'OIH', 'NCH'), feature_group_count=ping_count * channels, precision=lax.Precision.HIGHEST)
    return result.reshape(ping_count, channels, samples).astype(jnp.bfloat16)

def make_steer(first_row, row_count, track, channels, scaling, spread):
    xpos = jnp.asarray(first_row).astype(jnp.float32) + jnp.arange(row_count, dtype=jnp.float32)
    centre = track.astype(jnp.float32)[:, None] + 0.5 * jnp.arange(channels, dtype=jnp.float32)[None, :]
    centre = centre.reshape(-1)
    diff = xpos[:, None] - centre[None, :]
    dist = diff * (8.0 / X)
    weight = jnp.exp(-0.5 * dist * dist) * scaling
    phase = diff * diff * (math.pi / spread)
    return ((weight * jnp.cos(phase)).astype(jnp.bfloat16), (weight * jnp.sin(phase)).astype(jnp.bfloat16))

def reference(echoes, band_offset, sway_delay, channel_gain, track_bin):
    taps = make_taps(sway_delay, channel_gain)
    scaling = 1.0 / math.sqrt(PINGS * C)
    band_count = RANGE // R_DEV
    groups = (echoes.reshape(N_PING, PING_DEV, C, RANGE), band_offset.reshape(N_PING, PING_DEV), taps.reshape(N_PING, PING_DEV, C, BAND), track_bin.reshape(N_PING, PING_DEV))

    def add_group(totals, pieces):
        echo_group, offset_group, taps_group, track_group = pieces
        padded = jnp.pad(echo_group, ((0, 0), (0, 0), (HALO, HALO)))
        compensated = compensate(padded, offset_group, taps_group, RANGE)
        columns_all = compensated.reshape(PING_DEV * C, RANGE)

        def one_band(band):
            spread = 0.5 * X * (1.0 + (band.astype(jnp.float32) + 0.5) * (R_DEV / RANGE))
            steer_real, steer_imag = make_steer(0, X, track_group, C, scaling, spread)
            columns = lax.dynamic_slice_in_dim(columns_all, (band * R_DEV).astype(jnp.int32), R_DEV, 1)
            part_real = jnp.dot(steer_real, columns, preferred_element_type=jnp.float32).astype(jnp.bfloat16)
            part_imag = jnp.dot(steer_imag, columns, preferred_element_type=jnp.float32).astype(jnp.bfloat16)
            return (part_real, part_imag)
        band_real, band_imag = lax.map(one_band, jnp.arange(band_count, dtype=jnp.int32))
        band_real = lax.optimization_barrier(band_real)
        band_imag = lax.optimization_barrier(band_imag)
        part_real = jnp.transpose(band_real.astype(jnp.float32), (1, 0, 2)).reshape(X, RANGE)
        part_imag = jnp.transpose(band_imag.astype(jnp.float32), (1, 0, 2)).reshape(X, RANGE)
        return ((totals[0] + part_real, totals[1] + part_imag), None)
    start = (jnp.zeros((X, RANGE), jnp.float32), jnp.zeros((X, RANGE), jnp.float32))
    images, _ = lax.scan(add_group, start, groups)
    return (images[0], images[1])
```

```python
import functools
import math

import jax
import jax.numpy as jnp
import numpy as np
from jax import lax
from jax.experimental import pallas as pl
from jax.experimental.pallas import tpu as pltpu
from jax.sharding import PartitionSpec as P

X = 2048
BAND = 64
HALO = 128
NR = 32
NP = 16
PD = 8
C = 32
RD = 128
PC = PD * C
ROWS = X // NP
NC = 2
PR = PC // NC
MESH = pl.DeviceIdType.MESH


def fit(fun, degree):
    nodes = 0.125 + 0.125 * np.cos(np.pi * (np.arange(400) + 0.5) / 400)
    series = np.polynomial.chebyshev.Chebyshev.fit(nodes, fun(nodes), degree, domain=[0.0, 0.25])
    return [float(c) for c in series.convert(kind=np.polynomial.Polynomial).coef]


COS = fit(lambda w: np.cos(2 * np.pi * np.sqrt(w)), 8)
SIN = fit(lambda w: np.sin(2 * np.pi * np.sqrt(w)) / np.sqrt(w), 7)
SINPI = fit(lambda w: np.sin(np.pi * np.sqrt(w)) / np.sqrt(w), 6)


def horner(coefs, w):
    value = jnp.full_like(w, coefs[-1])
    for c in coefs[-2::-1]:
        value = value * w + c
    return value


def sin_pi(u):
    u = jnp.minimum(u, 1.0 - u)
    return u * horner(SINPI, u * u)


def kernel(
    off_ref, track_ref, e_ref, sway_ref, gain_ref, re_ref, im_ref,
    halo, et, win, taps, gath, mine, steer, acc,
    hs, hr, ms, mr, ss, rs,
):
    r = lax.axis_index("range")
    g = lax.axis_index("ping")
    z, core = g // 2, g % 2
    half, pos = z // 4, z % 4
    other = (r, g + 1 - 2 * core)
    right = (r, jnp.minimum(g + 2, NP - 1))
    left = (r, jnp.maximum(g - 2, 0))
    across = (r, g + 8 - 16 * half)
    after = (jnp.minimum(r + 1, NR - 1), g)
    before = (jnp.maximum(r - 1, 0), g)

    barrier = pltpu.get_barrier_semaphore()
    for j in range(1, NP):
        pl.semaphore_signal(barrier, 1, device_id=(r, (g + j) % NP), device_id_type=MESH)

    @pl.when(r > 0)
    def _():
        pl.semaphore_signal(barrier, 1, device_id=before, device_id_type=MESH)

    @pl.when(r < NR - 1)
    def _():
        pl.semaphore_signal(barrier, 1, device_id=after, device_id_type=MESH)

    lane = lax.broadcasted_iota(jnp.int32, (8, PC), 1)
    ping = lane // C
    centre = lane % C
    for p in range(PD):
        centre = centre + jnp.where(ping == p, 2 * track_ref[p], 0)
    mine[g] = centre

    kpos = lax.broadcasted_iota(jnp.int32, (BAND, 1), 0).astype(jnp.float32)
    edge = sin_pi((kpos + 0.5) * (1.0 / BAND))
    edge = edge * edge
    kfull = lax.broadcasted_iota(jnp.int32, (BAND, 128), 0)
    odd = (kfull % 2).astype(jnp.float32)
    for b in range(2):
        sway = jnp.concatenate([sway_ref[4 * b + q : 4 * b + q + 1, :] for q in range(4)], axis=1)
        gain = jnp.concatenate([gain_ref[4 * b + q : 4 * b + q + 1, :] for q in range(4)], axis=1)
        top = sin_pi(sway) * (1.0 / math.pi)
        shift = kfull.astype(jnp.float32) - (BAND / 2 - 1) - sway
        sinc = jnp.where(shift == 0.0, 1.0, (1.0 - 2.0 * odd) * top / jnp.where(shift == 0.0, 1.0, shift))
        taps[b] = sinc * edge * gain

    pl.semaphore_wait(barrier, NP + 1 - 1 // (r + 1) - r // (NR - 1))

    def halo_copy(way, device):
        return pltpu.make_async_remote_copy(
            e_ref, halo.at[way], hs.at[way], hr.at[way], device_id=device, device_id_type=MESH
        )

    @pl.when(r < NR - 1)
    def _():
        halo_copy(0, after).start()

    @pl.when(r > 0)
    def _():
        halo_copy(1, before).start()

    def mine_copy(slot, j):
        return pltpu.make_async_remote_copy(
            mine.at[slot], mine.at[slot], ms.at[j], mr.at[slot], device_id=(r, (g + j) % NP), device_id_type=MESH
        )

    for j in range(1, NP):
        mine_copy(g, j).start()

    def lay(block, third):
        for b in range(2):
            et[b, third * RD : (third + 1) * RD, :] = block[b * 128 : (b + 1) * 128, :].astype(jnp.float32).T

    lay(e_ref, 1)

    full = (64 * 2 * (2 * r + 65)).astype(jnp.float32)
    turn = 1.0 / jnp.full((16, PC), full, jnp.float32)
    row = 2 * (ROWS * g + lax.broadcasted_iota(jnp.int32, (16, PC), 0))
    scale = 1.0 / math.sqrt(NP * PC)

    def build(slot):
        def rows(i, carry):
            centres = jnp.concatenate([mine[slot], mine[slot]], axis=0)
            m = (row + 32 * i - centres).astype(jnp.float32)
            m2 = m * m
            u = (m2 - jnp.floor(m2 * turn + 0.5) * full) * turn
            w = u * u
            weight = jnp.exp(m2 * (-1.0 / (8.0 * 65536.0))) * scale
            at = pl.multiple_of(16 * i, 16)
            steer[slot, pl.ds(at, 16), :] = (weight * horner(COS, w)).astype(jnp.bfloat16)
            at = pl.multiple_of(16 * i + ROWS, 16)
            steer[slot, pl.ds(at, 16), :] = (weight * (u * horner(SIN, w))).astype(jnp.bfloat16)
            return carry

        lax.fori_loop(0, ROWS // 16, rows, 0)

    build(g)

    @pl.when(r > 0)
    def _():
        halo_copy(0, after).wait_recv()
        lay(halo.at[0], 0)

    @pl.when(r == 0)
    def _():
        et[:, 0:RD, :] = jnp.zeros((2, RD, 128), jnp.float32)

    @pl.when(r < NR - 1)
    def _():
        halo_copy(1, before).wait_recv()
        lay(halo.at[1], 2)

    @pl.when(r == NR - 1)
    def _():
        et[:, 2 * RD : 3 * RD, :] = jnp.zeros((2, RD, 128), jnp.float32)

    def copy(slot, piece, way, device):
        part = pl.ds(piece * PR, PR)
        return pltpu.make_async_remote_copy(
            gath.at[slot, part], gath.at[slot, part], ss.at[slot, piece, way], rs.at[slot, piece],
            device_id=device, device_id_type=MESH,
        )

    def send(slot, piece, entry, own):
        @pl.when((pos < 3) & (entry <= pos))
        def _():
            copy(slot, piece, 0, right).start()

        @pl.when((pos > 0) & (entry >= pos))
        def _():
            copy(slot, piece, 1, left).start()

        if own:
            copy(slot, piece, 2, across).start()
        copy(slot, piece, 3, other).start()

    quarter = lax.broadcasted_iota(jnp.int32, (BAND + RD, 128), 1) // C
    for b in range(2):
        picked = et[b, pl.ds(off_ref[4 * b] + HALO, BAND + RD), :]
        for q in range(1, 4):
            picked = jnp.where(quarter == q, et[b, pl.ds(off_ref[4 * b + q] + HALO, BAND + RD), :], picked)
        win[...] = picked
        for t in range(2):
            total = [jnp.zeros((8, 128), jnp.float32) for _ in range(8)]
            for k in range(BAND):
                tap = taps[b, pl.ds(k, 8, stride=0), :]
                for i in range(8):
                    total[i] = total[i] + tap * win[64 * t + 8 * i + k : 64 * t + 8 * i + k + 8, :]
            acc[64 * t : 64 * t + 64, :] = jnp.concatenate(total, axis=0)
        gath[g, b * 128 : (b + 1) * 128, :] = acc[0:RD, :].T.astype(jnp.bfloat16)
        send(g, b, pos, True)

    def add(slot, first=False):
        part = jnp.dot(steer[slot], gath[slot], preferred_element_type=jnp.float32)
        acc[...] = part if first else acc[...] + part

    add(g, True)

    def near(i):
        return (jnp.abs(pos - 1), 2 + pos // 2 - 2 * (pos // 3), 3 * (1 - pos // 2))[i]

    events = [(0, near(i)) for i in range(3)] + [(1, pos)] + [(1, near(i)) for i in range(3)]
    chips = [4 * (half if o == 0 else 1 - half) + entry for o, entry in events]

    def ready(slot):
        mine_copy(slot, 1).wait_recv()
        build(slot)

    ready(2 * z + 1 - core)

    def partner(chip):
        slot = 2 * chip + 1 - core
        for piece in range(NC):
            copy(slot, piece, 3, other).wait_recv()
        add(slot)

    previous = z
    for (o, entry), chip in zip(events, chips):
        slot = 2 * chip + core
        ready(slot)
        ready(2 * chip + 1 - core)
        for piece in range(NC):
            copy(slot, piece, 3, other).wait_recv()
            send(slot, piece, entry, False)
        partner(previous)
        add(slot)
        previous = chip
    partner(previous)

    re_ref[...] = acc[0:ROWS, :]
    im_ref[...] = acc[ROWS : 2 * ROWS, :]

    @pl.when(r < NR - 1)
    def _():
        halo_copy(0, after).wait_send()

    @pl.when(r > 0)
    def _():
        halo_copy(1, before).wait_send()

    for j in range(1, NP):
        mine_copy(g, j).wait_send()

    for (o, entry), chip in zip([(0, pos)] + events, [z] + chips):
        slot = 2 * chip + core
        for piece in range(NC):

            @pl.when((pos < 3) & (entry <= pos))
            def _():
                copy(slot, piece, 0, right).wait_send()

            @pl.when((pos > 0) & (entry >= pos))
            def _():
                copy(slot, piece, 1, left).wait_send()

            if chip is z:
                copy(slot, piece, 2, across).wait_send()
            copy(slot, piece, 3, other).wait_send()


def shards(echoes, band_offset, sway_delay, channel_gain, track_bin):
    whole = pl.BlockSpec(memory_space=pltpu.VMEM)
    scalars = pl.BlockSpec(memory_space=pltpu.SMEM)
    out = jax.ShapeDtypeStruct((ROWS, RD), jnp.float32)
    return pl.pallas_call(
        kernel,
        out_shape=(out, out),
        in_specs=[scalars, scalars, whole, whole, whole],
        out_specs=(whole, whole),
        scratch_shapes=[
            pltpu.VMEM((2, PC, RD), jnp.bfloat16),
            pltpu.VMEM((2, 3 * RD, 128), jnp.float32),
            pltpu.VMEM((BAND + RD, 128), jnp.float32),
            pltpu.VMEM((2, BAND, 128), jnp.float32),
            pltpu.VMEM((NP, PC, RD), jnp.bfloat16),
            pltpu.VMEM((NP, 8, PC), jnp.int32),
            pltpu.VMEM((NP, 2 * ROWS, PC), jnp.bfloat16),
            pltpu.VMEM((2 * ROWS, RD), jnp.float32),
            pltpu.SemaphoreType.DMA((2,)),
            pltpu.SemaphoreType.DMA((2,)),
            pltpu.SemaphoreType.DMA((NP,)),
            pltpu.SemaphoreType.DMA((NP,)),
            pltpu.SemaphoreType.DMA((NP, NC, 4)),
            pltpu.SemaphoreType.DMA((NP, NC)),
        ],
        compiler_params=pltpu.CompilerParams(collective_id=0, has_side_effects=True),
    )(band_offset, track_bin, echoes.reshape(PC, RD), sway_delay, channel_gain)


def solution(mesh):
    return jax.shard_map(
        shards,
        mesh=mesh,
        in_specs=(P("ping", None, "range"), P("ping"), P("ping", None), P("ping", None), P("ping")),
        out_specs=(P("ping", "range"), P("ping", "range")),
        check_vma=False,
    )
```

```python
import functools
import math

import jax
import jax.numpy as jnp
import numpy as np
from jax import lax
from jax.experimental import pallas as pl
from jax.experimental.pallas import tpu as pltpu
from jax.sharding import PartitionSpec as P

X = 2048
BAND = 64
HALO = 128
NR = 32
NP = 16
PD = 8
C = 32
RD = 128
PC = PD * C
ROWS = X // NP
GROUP = 8
NC = 2
PR = RD // NC
MESH = pl.DeviceIdType.MESH


def fit(fun, degree):
    nodes = 0.125 + 0.125 * np.cos(np.pi * (np.arange(400) + 0.5) / 400)
    series = np.polynomial.chebyshev.Chebyshev.fit(nodes, fun(nodes), degree, domain=[0.0, 0.25])
    return [float(c) for c in series.convert(kind=np.polynomial.Polynomial).coef]


COS = fit(lambda w: np.cos(2 * np.pi * np.sqrt(w)), 8)
SIN = fit(lambda w: np.sin(2 * np.pi * np.sqrt(w)) / np.sqrt(w), 7)
SINPI = fit(lambda w: np.sin(np.pi * np.sqrt(w)) / np.sqrt(w), 6)


def horner(coefs, w):
    value = jnp.full_like(w, coefs[-1])
    for c in coefs[-2::-1]:
        value = value * w + c
    return value


def sin_pi(u):
    u = jnp.minimum(u, 1.0 - u)
    return u * horner(SINPI, u * u)


def kernel(
    off_ref, track_ref, e_ref, sway_ref, gain_ref, re_ref, im_ref,
    halo, et, win, taps, mine, gath, steer, acc, out_a, out_b, in_a, in_b,
    hs, hr, ms, mr, ss, rs, xs, xr, bs, br,
):
    r = lax.axis_index("range")
    g = lax.axis_index("ping")
    y = r % 4
    half, q = g // GROUP, g % GROUP
    pos, core = q // 2, q % 2
    base = GROUP * half
    across = (r, g + GROUP - 2 * GROUP * half)
    after = (jnp.minimum(r + 1, NR - 1), g)
    before = (jnp.maximum(r - 1, 0), g)
    crossing = 1 // (y + 1) - 1 // (r + 1) + y // 3 - r // (NR - 1)
    beyond = jnp.clip(r - 1 + 2 * (y // 3), 0, NR - 1)
    far = ((beyond, g), (beyond, g + GROUP - 2 * GROUP * half))

    barrier = pltpu.get_barrier_semaphore()

    def greet(device):
        pl.semaphore_signal(barrier, 1, device_id=device, device_id_type=MESH)

    @pl.when(crossing == 1)
    def _():
        greet(far[0])
        greet(far[1])

    for j in range(1, GROUP):
        greet((r, base + (q + j) % GROUP))
    greet(across)

    @pl.when(y > 0)
    def _():
        greet(before)

    @pl.when(y < 3)
    def _():
        greet(after)

    lane = lax.broadcasted_iota(jnp.int32, (1, PC), 1)
    centre = lane % C
    for p in range(PD):
        centre = centre + jnp.where(lane // C == p, 2 * track_ref[p], 0)
    mine[q] = centre

    kpos = lax.broadcasted_iota(jnp.int32, (BAND, 1), 0).astype(jnp.float32)
    edge = sin_pi((kpos + 0.5) * (1.0 / BAND))
    edge = edge * edge
    kfull = lax.broadcasted_iota(jnp.int32, (BAND, 128), 0)
    odd = (kfull % 2).astype(jnp.float32)
    for b in range(2):
        sway = jnp.concatenate([sway_ref[4 * b + i : 4 * b + i + 1, :] for i in range(4)], axis=1)
        gain = jnp.concatenate([gain_ref[4 * b + i : 4 * b + i + 1, :] for i in range(4)], axis=1)
        top = sin_pi(sway) * (1.0 / math.pi)
        shift = kfull.astype(jnp.float32) - (BAND / 2 - 1) - sway
        sinc = jnp.where(shift == 0.0, 1.0, (1.0 - 2.0 * odd) * top / jnp.where(shift == 0.0, 1.0, shift))
        taps[b] = sinc * edge * gain

    zeros = jnp.zeros((RD, 128), jnp.float32)

    def lay(block, kind, third):
        for b in range(2):
            et[kind, b, third * RD : (third + 1) * RD, :] = block[b * 128 : (b + 1) * 128, :].astype(jnp.float32).T

    def blank(kind, third):
        for b in range(2):
            et[kind, b, third * RD : (third + 1) * RD, :] = zeros

    quarter = lax.broadcasted_iota(jnp.int32, (BAND + RD, 128), 1) // C

    def align(kind):
        for b in range(2):
            picked = et[kind, b, pl.ds(off_ref[4 * b] + HALO, BAND + RD), :]
            for i in range(1, 4):
                picked = jnp.where(quarter == i, et[kind, b, pl.ds(off_ref[4 * b + i] + HALO, BAND + RD), :], picked)
            win[b] = picked

    def filtered(kind, piece):
        for b in range(2):
            total = [jnp.zeros((8, 128), jnp.float32) for _ in range(PR // 8)]
            for k in range(BAND):
                tap = taps[b, pl.ds(k, 8, stride=0), :]
                for i in range(PR // 8):
                    at = PR * piece + 8 * i + k
                    total[i] = total[i] + tap * win[b, at : at + 8, :]
            block = jnp.concatenate(total, axis=0).astype(jnp.bfloat16)
            gath[kind, q, piece * PR : (piece + 1) * PR, b * 128 : (b + 1) * 128] = block

    lay(e_ref, 0, 1)
    blank(1, 1)

    @pl.when(y == 3)
    def _():
        lay(e_ref, 1, 0)
        blank(1, 2)

    @pl.when(y == 0)
    def _():
        blank(1, 0)
        lay(e_ref, 1, 2)

    @pl.when(crossing == 1)
    def _():
        align(1)
        for piece in range(NC):
            filtered(1, piece)

    pl.semaphore_wait(barrier, GROUP + 2 - 1 // (y + 1) - y // 3 + 2 * crossing)

    def halo_copy(way, device):
        return pltpu.make_async_remote_copy(
            e_ref, halo.at[way], hs.at[way], hr.at[way], device_id=device, device_id_type=MESH
        )

    @pl.when(y < 3)
    def _():
        halo_copy(0, after).start()

    @pl.when(y > 0)
    def _():
        halo_copy(1, before).start()

    def mine_copy(slot, j):
        return pltpu.make_async_remote_copy(
            mine.at[slot], mine.at[slot], ms.at[j], mr.at[slot],
            device_id=(r, base + (q + j) % GROUP), device_id_type=MESH,
        )

    for j in range(1, GROUP):
        mine_copy(q, j).start()

    def copy(kind, slot, piece, way):
        rows = pl.ds(piece * PR, PR)
        peer = q + 1 - 2 * core if way == 0 else (q + 2 * way) % GROUP
        return pltpu.make_async_remote_copy(
            gath.at[kind, slot, rows], gath.at[kind, slot, rows], ss.at[kind, slot, piece, way], rs.at[kind, slot, piece],
            device_id=(r, base + peer), device_id_type=MESH,
        )

    def spread(kind, piece):
        for way in (2, 1, 3, 0):
            copy(kind, q, piece, way).start()

    @pl.when(crossing == 1)
    def _():
        for piece in range(NC):
            spread(1, piece)

    @pl.when(y > 0)
    def _():
        halo_copy(0, after).wait_recv()
        lay(halo.at[0], 0, 0)

    @pl.when(y == 0)
    def _():
        blank(0, 0)

    @pl.when(y < 3)
    def _():
        halo_copy(1, before).wait_recv()
        lay(halo.at[1], 0, 2)

    @pl.when(y == 3)
    def _():
        blank(0, 2)

    align(0)
    for piece in range(NC):
        filtered(0, piece)
        spread(0, piece)

    scale = 1.0 / math.sqrt(NP * PC)

    def build(kind, slot, band):
        full = (64 * 2 * (2 * band + 65)).astype(jnp.float32)
        turn = 1.0 / jnp.full((16, PC), full, jnp.float32)
        row = 2 * lax.broadcasted_iota(jnp.int32, (16, PC), 0)
        from_centre = row - jnp.broadcast_to(mine[slot], (16, PC))

        def rows(i, carry):
            first = g + (i // 8) * (GROUP - 2 * GROUP * half)
            m = (from_centre + (2 * ROWS * first + 32 * (i % 8))).astype(jnp.float32)
            m2 = m * m
            u = (m2 - jnp.floor(m2 * turn + 0.5) * full) * turn
            w = u * u
            weight = jnp.exp(m2 * (-1.0 / (8.0 * 65536.0))) * scale
            at = 2 * ROWS * (i // 8) + 16 * (i % 8)
            steer[kind, slot, pl.ds(pl.multiple_of(at, 16), 16), :] = (weight * horner(COS, w)).astype(jnp.bfloat16)
            at = at + ROWS
            steer[kind, slot, pl.ds(pl.multiple_of(at, 16), 16), :] = (weight * (u * horner(SIN, w))).astype(
                jnp.bfloat16
            )
            return carry

        lax.fori_loop(0, 2 * ROWS // 16, rows, 0)

    def slots(way):
        return (q + 2 * way) % GROUP

    twin = q + 1 - 2 * core
    order = [q, twin] + [s for way in (1, 3, 2) for s in (slots(way), (twin + 2 * way) % GROUP)]

    for i, slot in enumerate(order):
        if i:
            mine_copy(slot, 1).wait_recv()

        @pl.when(crossing == 1)
        def _():
            build(1, slot, beyond)

        build(0, slot, r)

    def add(kind, slot, piece, first=False):
        part = lax.dot_general(
            gath[kind, slot, piece * PR : (piece + 1) * PR, :], steer[kind, slot],
            (((1,), (1,)), ((), ())), preferred_element_type=jnp.float32,
        )
        rows = slice(piece * PR, (piece + 1) * PR)
        acc[rows, :] = part if first else acc[rows, :] + part

    def gather(kind, piece):
        add(kind, q, piece, True)
        for way in (1, 3, 2):
            copy(kind, slots(way), piece, 0).wait_recv()
            copy(kind, slots(way), piece, 0).start()
            add(kind, slots(way), piece)
        for way in (0, 1, 3, 2):
            slot = (twin + 2 * way) % GROUP
            copy(kind, slot, piece, 0).wait_recv()
            add(kind, slot, piece)

    def across_copy(piece):
        return pltpu.make_async_remote_copy(
            out_a.at[piece], in_a.at[piece], xs.at[piece], xr.at[piece], device_id=across, device_id_type=MESH
        )

    def far_copy(piece, which):
        return pltpu.make_async_remote_copy(
            out_b.at[which, piece], in_b.at[which, piece], bs.at[which, piece], br.at[which, piece],
            device_id=far[which], device_id_type=MESH,
        )

    W = 2 * ROWS

    @pl.when(crossing == 1)
    def _():
        for piece in range(NC):
            gather(1, piece)
            for which in range(2):
                out_b[which, piece] = acc[piece * PR : (piece + 1) * PR, which * W : (which + 1) * W].astype(jnp.bfloat16)
                far_copy(piece, which).start()

    for piece in range(NC):
        gather(0, piece)
        out_a[piece] = acc[piece * PR : (piece + 1) * PR, W : 2 * W].astype(jnp.bfloat16)
        across_copy(piece).start()

    for piece in range(NC):
        rows = slice(piece * PR, (piece + 1) * PR)
        across_copy(piece).wait_recv()
        acc[rows, 0:W] = acc[rows, 0:W] + in_a[piece].astype(jnp.float32)

        @pl.when(crossing == 1)
        def _():
            for which in range(2):
                far_copy(piece, which).wait_recv()
                acc[rows, 0:W] = acc[rows, 0:W] + in_b[which, piece].astype(jnp.float32)

    re_ref[...] = acc[:, 0:ROWS].T
    im_ref[...] = acc[:, ROWS : 2 * ROWS].T

    @pl.when(y < 3)
    def _():
        halo_copy(0, after).wait_send()

    @pl.when(y > 0)
    def _():
        halo_copy(1, before).wait_send()

    for j in range(1, GROUP):
        mine_copy(q, j).wait_send()

    def left(kind):
        for piece in range(NC):
            for way in range(4):
                copy(kind, q, piece, way).wait_send()
                if way:
                    copy(kind, slots(way), piece, 0).wait_send()

    left(0)
    for piece in range(NC):
        across_copy(piece).wait_send()

    @pl.when(crossing == 1)
    def _():
        left(1)
        for piece in range(NC):
            for which in range(2):
                far_copy(piece, which).wait_send()


def shards(echoes, band_offset, sway_delay, channel_gain, track_bin):
    whole = pl.BlockSpec(memory_space=pltpu.VMEM)
    scalars = pl.BlockSpec(memory_space=pltpu.SMEM)
    out = jax.ShapeDtypeStruct((ROWS, RD), jnp.float32)
    dma = pltpu.SemaphoreType.DMA
    return pl.pallas_call(
        kernel,
        out_shape=(out, out),
        in_specs=[scalars, scalars, whole, whole, whole],
        out_specs=(whole, whole),
        scratch_shapes=[
            pltpu.VMEM((2, PC, RD), jnp.bfloat16),
            pltpu.VMEM((2, 2, 3 * RD, 128), jnp.float32),
            pltpu.VMEM((2, BAND + RD, 128), jnp.float32),
            pltpu.VMEM((2, BAND, 128), jnp.float32),
            pltpu.VMEM((GROUP, 1, PC), jnp.int32),
            pltpu.VMEM((2, GROUP, RD, PC), jnp.bfloat16),
            pltpu.VMEM((2, GROUP, 4 * ROWS, PC), jnp.bfloat16),
            pltpu.VMEM((RD, 4 * ROWS), jnp.float32),
            pltpu.VMEM((NC, PR, 2 * ROWS), jnp.bfloat16),
            pltpu.VMEM((2, NC, PR, 2 * ROWS), jnp.bfloat16),
            pltpu.VMEM((NC, PR, 2 * ROWS), jnp.bfloat16),
            pltpu.VMEM((2, NC, PR, 2 * ROWS), jnp.bfloat16),
            dma((2,)),
            dma((2,)),
            dma((GROUP,)),
            dma((GROUP,)),
            dma((2, GROUP, NC, 4)),
            dma((2, GROUP, NC)),
            dma((NC,)),
            dma((NC,)),
            dma((2, NC)),
            dma((2, NC)),
        ],
        compiler_params=pltpu.CompilerParams(collective_id=0, has_side_effects=True),
    )(band_offset, track_bin, echoes.reshape(PC, RD), sway_delay, channel_gain)


def solution(mesh):
    return jax.shard_map(
        shards,
        mesh=mesh,
        in_specs=(P("ping", None, "range"), P("ping"), P("ping", None), P("ping", None), P("ping")),
        out_specs=(P("ping", "range"), P("ping", "range")),
        check_vma=False,
    )
```

```python
import functools
import math

import jax
import jax.numpy as jnp
import numpy as np
from jax import lax
from jax.experimental import pallas as pl
from jax.experimental.pallas import tpu as pltpu
from jax.sharding import PartitionSpec as P

X = 2048
BAND = 64
HALO = 128
NR = 32
NP = 16
PD = 8
C = 32
RD = 128
PC = PD * C
ROWS = X // NP
GROUP = 8
NC = 1
PR = RD // NC
MESH = pl.DeviceIdType.MESH


def fit(fun, degree):
    nodes = 0.125 + 0.125 * np.cos(np.pi * (np.arange(400) + 0.5) / 400)
    series = np.polynomial.chebyshev.Chebyshev.fit(nodes, fun(nodes), degree, domain=[0.0, 0.25])
    return [float(c) for c in series.convert(kind=np.polynomial.Polynomial).coef]


COS = fit(lambda w: np.cos(2 * np.pi * np.sqrt(w)), 8)
SIN = fit(lambda w: np.sin(2 * np.pi * np.sqrt(w)) / np.sqrt(w), 7)
SINPI = fit(lambda w: np.sin(np.pi * np.sqrt(w)) / np.sqrt(w), 6)


def horner(coefs, w):
    value = jnp.full_like(w, coefs[-1])
    for c in coefs[-2::-1]:
        value = value * w + c
    return value


def sin_pi(u):
    u = jnp.minimum(u, 1.0 - u)
    return u * horner(SINPI, u * u)


def kernel(
    off_ref, track_ref, e_ref, sway_ref, gain_ref, re_ref, im_ref,
    halo, et, win, taps, mine, own_b, gath, steer, acc, out_a, in_a,
    hs, hr, ms, mr, ss, rs, xs, xr, bs,
):
    r = lax.axis_index("range")
    g = lax.axis_index("ping")
    y = r % 4
    half, q = g // GROUP, g % GROUP
    pos, core = q // 2, q % 2
    base = GROUP * half
    across = (r, g + GROUP - 2 * GROUP * half)
    after = (jnp.minimum(r + 1, NR - 1), g)
    before = (jnp.maximum(r - 1, 0), g)
    crossing = 1 // (y + 1) - 1 // (r + 1) + y // 3 - r // (NR - 1)
    beyond = jnp.clip(r - 1 + 2 * (y // 3), 0, NR - 1)
    far = (beyond, g + GROUP - 2 * GROUP * half)

    barrier = pltpu.get_barrier_semaphore()

    def greet(device):
        pl.semaphore_signal(barrier, 1, device_id=device, device_id_type=MESH)

    @pl.when(crossing == 1)
    def _():
        greet(far)
        for j in range(1, GROUP):
            greet((r, GROUP - base + (q + j) % GROUP))

    greet(across)
    for j in range(1, GROUP):
        greet((r, base + (q + j) % GROUP))

    @pl.when(y > 0)
    def _():
        greet(before)

    @pl.when(y < 3)
    def _():
        greet(after)

    lane = lax.broadcasted_iota(jnp.int32, (1, PC), 1)
    centre = lane % C
    for p in range(PD):
        centre = centre + jnp.where(lane // C == p, 2 * track_ref[p], 0)
    mine[g] = centre

    kpos = lax.broadcasted_iota(jnp.int32, (BAND, 1), 0).astype(jnp.float32)
    edge = sin_pi((kpos + 0.5) * (1.0 / BAND))
    edge = edge * edge
    kfull = lax.broadcasted_iota(jnp.int32, (BAND, 128), 0)
    odd = (kfull % 2).astype(jnp.float32)
    for b in range(2):
        sway = jnp.concatenate([sway_ref[4 * b + i : 4 * b + i + 1, :] for i in range(4)], axis=1)
        gain = jnp.concatenate([gain_ref[4 * b + i : 4 * b + i + 1, :] for i in range(4)], axis=1)
        top = sin_pi(sway) * (1.0 / math.pi)
        shift = kfull.astype(jnp.float32) - (BAND / 2 - 1) - sway
        sinc = jnp.where(shift == 0.0, 1.0, (1.0 - 2.0 * odd) * top / jnp.where(shift == 0.0, 1.0, shift))
        taps[b] = sinc * edge * gain

    zeros = jnp.zeros((RD, 128), jnp.float32)

    def lay(block, kind, third):
        for b in range(2):
            et[kind, b, third * RD : (third + 1) * RD, :] = block[b * 128 : (b + 1) * 128, :].astype(jnp.float32).T

    def blank(kind, third):
        for b in range(2):
            et[kind, b, third * RD : (third + 1) * RD, :] = zeros

    quarter = lax.broadcasted_iota(jnp.int32, (BAND + RD, 128), 1) // C

    def align(kind):
        for b in range(2):
            picked = et[kind, b, pl.ds(off_ref[4 * b] + HALO, BAND + RD), :]
            for i in range(1, 4):
                picked = jnp.where(quarter == i, et[kind, b, pl.ds(off_ref[4 * b + i] + HALO, BAND + RD), :], picked)
            win[b] = picked

    def filtered(kind, piece):
        for b in range(2):
            total = [jnp.zeros((8, 128), jnp.float32) for _ in range(PR // 8)]
            for k in range(BAND):
                tap = taps[b, pl.ds(k, 8, stride=0), :]
                for i in range(PR // 8):
                    at = PR * piece + 8 * i + k
                    total[i] = total[i] + tap * win[b, at : at + 8, :]
            block = jnp.concatenate(total, axis=0).astype(jnp.bfloat16)
            rows, lanes = slice(piece * PR, (piece + 1) * PR), slice(b * 128, (b + 1) * 128)
            if kind:
                own_b[rows, lanes] = block
            else:
                gath[0, q, rows, lanes] = block

    lay(e_ref, 0, 1)
    blank(1, 1)

    @pl.when(y == 3)
    def _():
        lay(e_ref, 1, 0)
        blank(1, 2)

    @pl.when(y == 0)
    def _():
        blank(1, 0)
        lay(e_ref, 1, 2)

    @pl.when(crossing == 1)
    def _():
        align(1)
        for piece in range(NC):
            filtered(1, piece)

    pl.semaphore_wait(barrier, GROUP + 2 - 1 // (y + 1) - y // 3 + GROUP * crossing)

    def halo_copy(way, device):
        return pltpu.make_async_remote_copy(
            e_ref, halo.at[way], hs.at[way], hr.at[way], device_id=device, device_id_type=MESH
        )

    @pl.when(y < 3)
    def _():
        halo_copy(0, after).start()

    @pl.when(y > 0)
    def _():
        halo_copy(1, before).start()

    def mine_copy(group, there, j):
        return pltpu.make_async_remote_copy(
            mine.at[group], mine.at[group], ms.at[there, j], mr.at[group],
            device_id=(r, base + there * (GROUP - 2 * base) + (q + j) % GROUP), device_id_type=MESH,
        )

    def far_copy(piece):
        rows = pl.ds(piece * PR, PR)
        return pltpu.make_async_remote_copy(
            own_b.at[rows], gath.at[1, q, rows], bs.at[piece], rs.at[1, q, piece], device_id=far, device_id_type=MESH
        )

    @pl.when(crossing == 1)
    def _():
        for piece in range(NC):
            far_copy(piece).start()
        for j in range(GROUP):
            mine_copy(g, 1, j).start()

    for j in range(1, GROUP):
        mine_copy(g, 0, j).start()

    def copy(kind, slot, piece, way):
        rows = pl.ds(piece * PR, PR)
        peer = q + 1 - 2 * core if way == 0 else (q + 2 * way) % GROUP
        return pltpu.make_async_remote_copy(
            gath.at[kind, slot, rows], gath.at[kind, slot, rows], ss.at[kind, slot, piece, way], rs.at[kind, slot, piece],
            device_id=(r, base + peer), device_id_type=MESH,
        )

    def spread(kind, piece):
        for way in (2, 1, 3, 0):
            copy(kind, q, piece, way).start()

    @pl.when(y > 0)
    def _():
        halo_copy(0, after).wait_recv()
        lay(halo.at[0], 0, 0)

    @pl.when(y == 0)
    def _():
        blank(0, 0)

    @pl.when(y < 3)
    def _():
        halo_copy(1, before).wait_recv()
        lay(halo.at[1], 0, 2)

    @pl.when(y == 3)
    def _():
        blank(0, 2)

    align(0)
    for piece in range(NC):
        filtered(0, piece)
        spread(0, piece)

    scale = 1.0 / math.sqrt(NP * PC)

    def group_of(kind, slot):
        return slot + base + kind * (GROUP - 2 * base)

    def build(kind, slot):
        full = (64 * 2 * (2 * r + 65)).astype(jnp.float32)
        turn = 1.0 / jnp.full((16, PC), full, jnp.float32)
        row = 2 * lax.broadcasted_iota(jnp.int32, (16, PC), 0)
        from_centre = row - jnp.broadcast_to(mine[group_of(kind, slot)], (16, PC))

        def rows(i, carry):
            first = g + (i // 8) * (GROUP - 2 * GROUP * half)
            m = (from_centre + (2 * ROWS * first + 32 * (i % 8))).astype(jnp.float32)
            m2 = m * m
            u = (m2 - jnp.floor(m2 * turn + 0.5) * full) * turn
            w = u * u
            weight = jnp.exp(m2 * (-1.0 / (8.0 * 65536.0))) * scale
            at = 2 * ROWS * (i // 8) + 16 * (i % 8)
            steer[kind, slot, pl.ds(pl.multiple_of(at, 16), 16), :] = (weight * horner(COS, w)).astype(jnp.bfloat16)
            at = at + ROWS
            steer[kind, slot, pl.ds(pl.multiple_of(at, 16), 16), :] = (weight * (u * horner(SIN, w))).astype(
                jnp.bfloat16
            )
            return carry

        lax.fori_loop(0, 2 * ROWS // 16, rows, 0)

    def slots(way):
        return (q + 2 * way) % GROUP

    twin = q + 1 - 2 * core
    order = [q, twin] + [s for way in (1, 3, 2) for s in (slots(way), (twin + 2 * way) % GROUP)]

    for i, slot in enumerate(order):
        if i:
            mine_copy(group_of(0, slot), 0, 1).wait_recv()
        build(0, slot)

    def add(kind, slot, piece, first=False):
        part = lax.dot_general(
            gath[kind, slot, piece * PR : (piece + 1) * PR, :], steer[kind, slot],
            (((1,), (1,)), ((), ())), preferred_element_type=jnp.float32,
        )
        rows = slice(piece * PR, (piece + 1) * PR)
        acc[rows, :] = part if first else acc[rows, :] + part

    def arrive(kind, piece):
        for way in (1, 3, 2):
            copy(kind, slots(way), piece, 0).wait_recv()
            copy(kind, slots(way), piece, 0).start()

    def gather(kind, piece):
        for way in (0, 1, 3, 2):
            add(kind, slots(way), piece, kind == 0 and way == 0)
        for way in (0, 1, 3, 2):
            slot = (twin + 2 * way) % GROUP
            copy(kind, slot, piece, 0).wait_recv()
            add(kind, slot, piece)

    def across_copy(piece):
        return pltpu.make_async_remote_copy(
            out_a.at[piece], in_a.at[piece], xs.at[piece], xr.at[piece], device_id=across, device_id_type=MESH
        )

    W = 2 * ROWS

    def cross(piece):
        out_a[piece] = acc[piece * PR : (piece + 1) * PR, W : 2 * W].astype(jnp.bfloat16)
        across_copy(piece).start()

    for piece in range(NC):
        arrive(0, piece)

    @pl.when(crossing == 1)
    def _():
        for piece in range(NC):
            copy(1, q, piece, 0).wait_recv()
            spread(1, piece)

    for piece in range(NC):
        gather(0, piece)

        @pl.when(crossing == 0)
        def _():
            cross(piece)

    @pl.when(crossing == 1)
    def _():
        for slot in order:
            mine_copy(group_of(1, slot), 0, 1).wait_recv()
            build(1, slot)
        for piece in range(NC):
            arrive(1, piece)
        for piece in range(NC):
            gather(1, piece)
            cross(piece)

    for piece in range(NC):
        rows = slice(piece * PR, (piece + 1) * PR)
        across_copy(piece).wait_recv()
        acc[rows, 0:W] = acc[rows, 0:W] + in_a[piece].astype(jnp.float32)

    re_ref[...] = acc[:, 0:ROWS].T
    im_ref[...] = acc[:, ROWS : 2 * ROWS].T

    @pl.when(y < 3)
    def _():
        halo_copy(0, after).wait_send()

    @pl.when(y > 0)
    def _():
        halo_copy(1, before).wait_send()

    for j in range(1, GROUP):
        mine_copy(g, 0, j).wait_send()

    def left(kind):
        for piece in range(NC):
            for way in range(4):
                copy(kind, q, piece, way).wait_send()
                if way:
                    copy(kind, slots(way), piece, 0).wait_send()

    left(0)
    for piece in range(NC):
        across_copy(piece).wait_send()

    @pl.when(crossing == 1)
    def _():
        left(1)
        for piece in range(NC):
            far_copy(piece).wait_send()
        for j in range(GROUP):
            mine_copy(g, 1, j).wait_send()


def shards(echoes, band_offset, sway_delay, channel_gain, track_bin):
    whole = pl.BlockSpec(memory_space=pltpu.VMEM)
    scalars = pl.BlockSpec(memory_space=pltpu.SMEM)
    out = jax.ShapeDtypeStruct((ROWS, RD), jnp.float32)
    dma = pltpu.SemaphoreType.DMA
    return pl.pallas_call(
        kernel,
        out_shape=(out, out),
        in_specs=[scalars, scalars, whole, whole, whole],
        out_specs=(whole, whole),
        scratch_shapes=[
            pltpu.VMEM((2, PC, RD), jnp.bfloat16),
            pltpu.VMEM((2, 2, 3 * RD, 128), jnp.float32),
            pltpu.VMEM((2, BAND + RD, 128), jnp.float32),
            pltpu.VMEM((2, BAND, 128), jnp.float32),
            pltpu.VMEM((NP, 1, PC), jnp.int32),
            pltpu.VMEM((RD, PC), jnp.bfloat16),
            pltpu.VMEM((2, GROUP, RD, PC), jnp.bfloat16),
            pltpu.VMEM((2, GROUP, 4 * ROWS, PC), jnp.bfloat16),
            pltpu.VMEM((RD, 4 * ROWS), jnp.float32),
            pltpu.VMEM((NC, PR, 2 * ROWS), jnp.bfloat16),
            pltpu.VMEM((NC, PR, 2 * ROWS), jnp.bfloat16),
            dma((2,)),
            dma((2,)),
            dma((2, GROUP)),
            dma((NP,)),
            dma((2, GROUP, NC, 4)),
            dma((2, GROUP, NC)),
            dma((NC,)),
            dma((NC,)),
            dma((NC,)),
        ],
        compiler_params=pltpu.CompilerParams(collective_id=0, has_side_effects=True),
    )(band_offset, track_bin, echoes.reshape(PC, RD), sway_delay, channel_gain)


def solution(mesh):
    return jax.shard_map(
        shards,
        mesh=mesh,
        in_specs=(P("ping", None, "range"), P("ping"), P("ping", None), P("ping", None), P("ping")),
        out_specs=(P("ping", "range"), P("ping", "range")),
        check_vma=False,
    )
```

```python
import functools
import math

import jax
import jax.numpy as jnp
import numpy as np
from jax import lax
from jax.experimental import pallas as pl
from jax.experimental.pallas import tpu as pltpu
from jax.sharding import PartitionSpec as P

X = 2048
BAND = 64
HALO = 128
NR = 32
NP = 16
PD = 8
C = 32
RD = 128
PC = PD * C
ROWS = X // NP
GROUP = 8
NC = 1
PR = RD // NC
MESH = pl.DeviceIdType.MESH


def fit(fun, degree):
    nodes = 0.125 + 0.125 * np.cos(np.pi * (np.arange(400) + 0.5) / 400)
    series = np.polynomial.chebyshev.Chebyshev.fit(nodes, fun(nodes), degree, domain=[0.0, 0.25])
    return [float(c) for c in series.convert(kind=np.polynomial.Polynomial).coef]


COS = fit(lambda w: np.cos(2 * np.pi * np.sqrt(w)), 8)
SIN = fit(lambda w: np.sin(2 * np.pi * np.sqrt(w)) / np.sqrt(w), 7)
SINPI = fit(lambda w: np.sin(np.pi * np.sqrt(w)) / np.sqrt(w), 6)


def horner(coefs, w):
    value = jnp.full_like(w, coefs[-1])
    for c in coefs[-2::-1]:
        value = value * w + c
    return value


def sin_pi(u):
    u = jnp.minimum(u, 1.0 - u)
    return u * horner(SINPI, u * u)


def kernel(
    off_in, track_in, e_in, sway_in, gain_in, re_ref, im_ref,
    off_ref, track_ref, e_ref, sway_ref, gain_ref, loaded, halo, et, win, taps, mine, own_b, gath, steer, spin, head, acc, out_a, in_a,
    hs, hr, ms, mr, ss, rs, xs, xr, bs,
):
    r = lax.axis_index("range")
    g = lax.axis_index("ping")
    y = r % 4
    half, q = g // GROUP, g % GROUP
    pos, core = q // 2, q % 2
    base = GROUP * half
    across = (r, g + GROUP - 2 * GROUP * half)
    after = (jnp.minimum(r + 1, NR - 1), g)
    before = (jnp.maximum(r - 1, 0), g)
    crossing = 1 // (y + 1) - 1 // (r + 1) + y // 3 - r // (NR - 1)
    beyond = jnp.clip(r - 1 + 2 * (y // 3), 0, NR - 1)
    far = (beyond, g + GROUP - 2 * GROUP * half)

    pairs = ((track_in, track_ref), (off_in, off_ref), (e_in, e_ref), (sway_in, sway_ref), (gain_in, gain_ref))
    loads = [pltpu.make_async_copy(a, b, loaded.at[i]) for i, (a, b) in enumerate(pairs)]
    for load in loads:
        load.start()

    barrier = pltpu.get_barrier_semaphore()

    def greet(device):
        pl.semaphore_signal(barrier, 1, device_id=device, device_id_type=MESH)

    @pl.when(crossing == 1)
    def _():
        greet(far)

    greet(across)
    for j in range(1, GROUP):
        greet((r, base + (q + j) % GROUP))

    @pl.when(y > 0)
    def _():
        greet(before)

    @pl.when(y < 3)
    def _():
        greet(after)

    for load in loads:
        load.wait()

    lane = lax.broadcasted_iota(jnp.int32, (1, PC), 1)
    centre = lane % C
    for p in range(PD):
        centre = centre + jnp.where(lane // C == p, 2 * track_ref[p], 0)
    mine[g] = centre

    kpos = lax.broadcasted_iota(jnp.int32, (BAND, 1), 0).astype(jnp.float32)
    edge = sin_pi((kpos + 0.5) * (1.0 / BAND))
    edge = edge * edge
    kfull = lax.broadcasted_iota(jnp.int32, (BAND, 128), 0)
    odd = (kfull % 2).astype(jnp.float32)
    for b in range(2):
        sway = jnp.concatenate([sway_ref[4 * b + i : 4 * b + i + 1, :] for i in range(4)], axis=1)
        gain = jnp.concatenate([gain_ref[4 * b + i : 4 * b + i + 1, :] for i in range(4)], axis=1)
        top = sin_pi(sway) * (1.0 / math.pi)
        shift = kfull.astype(jnp.float32) - (BAND / 2 - 1) - sway
        sinc = jnp.where(shift == 0.0, 1.0, (1.0 - 2.0 * odd) * top / jnp.where(shift == 0.0, 1.0, shift))
        taps[b] = sinc * edge * gain

    zeros = jnp.zeros((RD, 128), jnp.float32)

    def lay(block, kind, third):
        for b in range(2):
            et[kind, b, third * RD : (third + 1) * RD, :] = block[b * 128 : (b + 1) * 128, :].astype(jnp.float32).T

    def blank(kind, third):
        for b in range(2):
            et[kind, b, third * RD : (third + 1) * RD, :] = zeros

    quarter = lax.broadcasted_iota(jnp.int32, (BAND + RD, 128), 1) // C

    def align(kind):
        for b in range(2):
            picked = et[kind, b, pl.ds(off_ref[4 * b] + HALO, BAND + RD), :]
            for i in range(1, 4):
                picked = jnp.where(quarter == i, et[kind, b, pl.ds(off_ref[4 * b + i] + HALO, BAND + RD), :], picked)
            win[b] = picked

    def filtered(kind, piece):
        for b in range(2):
            total = [jnp.zeros((8, 128), jnp.float32) for _ in range(PR // 8)]
            for k in range(BAND):
                tap = taps[b, pl.ds(k, 8, stride=0), :]
                for i in range(PR // 8):
                    at = PR * piece + 8 * i + k
                    total[i] = total[i] + tap * win[b, at : at + 8, :]
            block = jnp.concatenate(total, axis=0).astype(jnp.bfloat16)
            rows, lanes = slice(piece * PR, (piece + 1) * PR), slice(b * 128, (b + 1) * 128)
            if kind:
                own_b[rows, lanes] = block
            else:
                gath[0, q, rows, lanes] = block

    lay(e_ref, 0, 1)
    blank(1, 1)

    @pl.when(y == 3)
    def _():
        lay(e_ref, 1, 0)
        blank(1, 2)

    @pl.when(y == 0)
    def _():
        blank(1, 0)
        lay(e_ref, 1, 2)

    @pl.when(crossing == 1)
    def _():
        align(1)
        for piece in range(NC):
            filtered(1, piece)

    pl.semaphore_wait(barrier, GROUP + 2 - 1 // (y + 1) - y // 3 + crossing)

    def halo_copy(way, device):
        return pltpu.make_async_remote_copy(
            e_ref, halo.at[way], hs.at[way], hr.at[way], device_id=device, device_id_type=MESH
        )

    @pl.when(y < 3)
    def _():
        halo_copy(0, after).start()

    @pl.when(y > 0)
    def _():
        halo_copy(1, before).start()

    opposite = g + GROUP - 2 * base

    def mine_copy(group, kind, j):
        device = (r, base + (q + j) % GROUP) if j else across
        return pltpu.make_async_remote_copy(
            mine.at[group], mine.at[group], ms.at[kind, j], mr.at[group], device_id=device, device_id_type=MESH
        )

    def far_copy(piece):
        rows = pl.ds(piece * PR, PR)
        return pltpu.make_async_remote_copy(
            own_b.at[rows], gath.at[1, q, rows], bs.at[piece], rs.at[1, q, piece], device_id=far, device_id_type=MESH
        )

    @pl.when(crossing == 1)
    def _():
        for piece in range(NC):
            far_copy(piece).start()
        mine_copy(g, 1, 0).start()

    for j in range(1, GROUP):
        mine_copy(g, 0, j).start()

    def copy(kind, slot, piece, way):
        rows = pl.ds(piece * PR, PR)
        peer = q + 1 - 2 * core if way == 0 else (q + 2 * way) % GROUP
        return pltpu.make_async_remote_copy(
            gath.at[kind, slot, rows], gath.at[kind, slot, rows], ss.at[kind, slot, piece, way], rs.at[kind, slot, piece],
            device_id=(r, base + peer), device_id_type=MESH,
        )

    def spread(kind, piece):
        for way in (2, 1, 3, 0):
            copy(kind, q, piece, way).start()

    @pl.when(y > 0)
    def _():
        halo_copy(0, after).wait_recv()
        lay(halo.at[0], 0, 0)

    @pl.when(y == 0)
    def _():
        blank(0, 0)

    @pl.when(y < 3)
    def _():
        halo_copy(1, before).wait_recv()
        lay(halo.at[1], 0, 2)

    @pl.when(y == 3)
    def _():
        blank(0, 2)

    align(0)
    for piece in range(NC):
        filtered(0, piece)
        spread(0, piece)

    @pl.when(crossing == 1)
    def _():
        mine_copy(opposite, 1, 0).wait_recv()
        for j in range(1, GROUP):
            mine_copy(opposite, 1, j).start()

    scale = 1.0 / math.sqrt(NP * PC)

    def group_of(kind, slot):
        return slot + base + kind * (GROUP - 2 * base)

    full = (64 * 2 * (2 * r + 65)).astype(jnp.float32)

    def wave(squares, factor):
        turn = 1.0 / jnp.full(squares.shape, full, jnp.float32)
        u = (squares - jnp.floor(squares * turn + 0.5) * full) * turn
        w = u * u
        weight = jnp.exp(squares * (-1.0 / (8.0 * 65536.0))) * factor
        return weight * horner(COS, w), weight * (u * horner(SIN, w))

    eight = lax.broadcasted_iota(jnp.int32, (128, 128), 0)
    spin[0], spin[1] = wave((64 * (eight // 8) * (eight % 8)).astype(jnp.float32), 1.0)

    def build(kind, slot):
        centres = mine[group_of(kind, slot)]
        starts = [2 * ROWS * g - centres, 2 * ROWS * opposite - centres]
        step = lax.broadcasted_iota(jnp.int32, (16, PC), 0)
        n = jnp.concatenate([16 * step + start for start in starts], axis=0).astype(jnp.float32)
        head[0], head[1] = wave(n * n, scale)
        s8 = lax.broadcasted_iota(jnp.int32, (8, PC), 0)
        turned = jnp.concatenate([4 * s8 * (start + s8) for start in starts], axis=0).astype(jnp.float32)
        cos, sin = wave(turned, 1.0)
        for part in range(2):
            cos8, sin8 = cos[8 * part : 8 * part + 8], sin[8 * part : 8 * part + 8]

            for i in range(ROWS // 16):
                real, imag = [], []
                for j in range(2):
                    at = 16 * i + 8 * j
                    cr = jnp.concatenate([spin[0, at : at + 8, :]] * 2, axis=1)
                    ci = jnp.concatenate([spin[1, at : at + 8, :]] * 2, axis=1)
                    br, bi = cos8 * cr - sin8 * ci, cos8 * ci + sin8 * cr
                    hr = head[0, pl.ds(16 * part + 2 * i + j, 8, stride=0), :]
                    hi = head[1, pl.ds(16 * part + 2 * i + j, 8, stride=0), :]
                    real.append(hr * br - hi * bi)
                    imag.append(hr * bi + hi * br)
                at = 2 * ROWS * part + 16 * i
                steer[kind, slot, at : at + 16, :] = jnp.concatenate(real, axis=0).astype(jnp.bfloat16)
                at = at + ROWS
                steer[kind, slot, at : at + 16, :] = jnp.concatenate(imag, axis=0).astype(jnp.bfloat16)

    def build_all(kind):
        for i, slot in enumerate(order):
            if i:
                mine_copy(group_of(kind, slot), 0, 1).wait_recv()

        def one(slot, carry):
            build(kind, slot)
            return carry

        lax.fori_loop(0, GROUP, one, 0)

    def slots(way):
        return (q + 2 * way) % GROUP

    twin = q + 1 - 2 * core
    order = [q, twin] + [s for way in (1, 3, 2) for s in (slots(way), (twin + 2 * way) % GROUP)]

    build_all(0)

    def add(part, kind, slot, first=False):
        product = lax.dot_general(
            gath[kind, slot], steer[kind, slot, 2 * ROWS * part : 2 * ROWS * (part + 1), :],
            (((1,), (1,)), ((), ())), preferred_element_type=jnp.float32,
        )
        acc[part] = product if first else acc[part] + product

    def arrive(kind, piece):
        for way in (1, 3, 2):
            copy(kind, slots(way), piece, 0).wait_recv()
            copy(kind, slots(way), piece, 0).start()

    def outer(kind):
        for way in (0, 1, 3, 2):
            add(1, kind, slots(way), kind == 0 and way == 0)
        for way in (0, 1, 3, 2):
            slot = (twin + 2 * way) % GROUP
            for piece in range(NC):
                copy(kind, slot, piece, 0).wait_recv()
            add(1, kind, slot)

    def inner(kind):
        for i, slot in enumerate(order):
            add(0, kind, slot, kind == 0 and i == 0)

    across_copy = pltpu.make_async_remote_copy(
        out_a, in_a, xs.at[0], xr.at[0], device_id=across, device_id_type=MESH
    )

    def cross():
        out_a[...] = acc[1].astype(jnp.bfloat16)
        across_copy.start()

    for piece in range(NC):
        arrive(0, piece)

    @pl.when(crossing == 1)
    def _():
        for piece in range(NC):
            copy(1, q, piece, 0).wait_recv()
            spread(1, piece)
        build_all(1)

    outer(0)

    @pl.when(crossing == 0)
    def _():
        cross()

    inner(0)

    @pl.when(crossing == 1)
    def _():
        for piece in range(NC):
            arrive(1, piece)
        outer(1)
        cross()
        inner(1)

    across_copy.wait_recv()
    acc[0] = acc[0] + in_a[...].astype(jnp.float32)

    re_ref[...] = acc[0, :, 0:ROWS].T
    im_ref[...] = acc[0, :, ROWS : 2 * ROWS].T

    @pl.when(y < 3)
    def _():
        halo_copy(0, after).wait_send()

    @pl.when(y > 0)
    def _():
        halo_copy(1, before).wait_send()

    for j in range(1, GROUP):
        mine_copy(g, 0, j).wait_send()

    def left(kind):
        for piece in range(NC):
            for way in range(4):
                copy(kind, q, piece, way).wait_send()
                if way:
                    copy(kind, slots(way), piece, 0).wait_send()

    left(0)
    across_copy.wait_send()

    @pl.when(crossing == 1)
    def _():
        left(1)
        for piece in range(NC):
            far_copy(piece).wait_send()
        mine_copy(g, 1, 0).wait_send()
        for j in range(1, GROUP):
            mine_copy(opposite, 1, j).wait_send()


def shards(echoes, band_offset, sway_delay, channel_gain, track_bin):
    whole = pl.BlockSpec(memory_space=pltpu.VMEM)
    kept = pl.BlockSpec(memory_space=pltpu.HBM)
    out = jax.ShapeDtypeStruct((ROWS, RD), jnp.float32)
    dma = pltpu.SemaphoreType.DMA
    return pl.pallas_call(
        kernel,
        out_shape=(out, out),
        in_specs=[kept] * 5,
        out_specs=(whole, whole),
        scratch_shapes=[
            pltpu.SMEM((PD,), jnp.int32),
            pltpu.SMEM((PD,), jnp.int32),
            pltpu.VMEM((PC, RD), jnp.bfloat16),
            pltpu.VMEM((PD, C), jnp.float32),
            pltpu.VMEM((PD, C), jnp.float32),
            dma((5,)),
            pltpu.VMEM((2, PC, RD), jnp.bfloat16),
            pltpu.VMEM((2, 2, 3 * RD, 128), jnp.float32),
            pltpu.VMEM((2, BAND + RD, 128), jnp.float32),
            pltpu.VMEM((2, BAND, 128), jnp.float32),
            pltpu.VMEM((NP, 1, PC), jnp.int32),
            pltpu.VMEM((RD, PC), jnp.bfloat16),
            pltpu.VMEM((2, GROUP, RD, PC), jnp.bfloat16),
            pltpu.VMEM((2, GROUP, 4 * ROWS, PC), jnp.bfloat16),
            pltpu.VMEM((2, 128, 128), jnp.float32),
            pltpu.VMEM((2, 32, PC), jnp.float32),
            pltpu.VMEM((2, RD, 2 * ROWS), jnp.float32),
            pltpu.VMEM((RD, 2 * ROWS), jnp.bfloat16),
            pltpu.VMEM((RD, 2 * ROWS), jnp.bfloat16),
            dma((2,)),
            dma((2,)),
            dma((2, GROUP)),
            dma((NP,)),
            dma((2, GROUP, NC, 4)),
            dma((2, GROUP, NC)),
            dma((1,)),
            dma((1,)),
            dma((NC,)),
        ],
        compiler_params=pltpu.CompilerParams(collective_id=0, has_side_effects=True),
    )(band_offset, track_bin, echoes.reshape(PC, RD), sway_delay, channel_gain)


def solution(mesh):
    return jax.shard_map(
        shards,
        mesh=mesh,
        in_specs=(P("ping", None, "range"), P("ping"), P("ping", None), P("ping", None), P("ping")),
        out_specs=(P("ping", "range"), P("ping", "range")),
        check_vma=False,
    )
```

```python
import functools
import math

import jax
import jax.numpy as jnp
import numpy as np
from jax import lax
from jax.experimental import pallas as pl
from jax.experimental.pallas import tpu as pltpu
from jax.sharding import PartitionSpec as P

X = 2048
BAND = 64
HALO = 128
NR = 32
NP = 16
PD = 8
C = 32
RD = 128
PC = PD * C
ROWS = X // NP
GROUP = 8
NC = 1
PR = RD // NC
MESH = pl.DeviceIdType.MESH


def fit(fun, degree):
    nodes = 0.125 + 0.125 * np.cos(np.pi * (np.arange(400) + 0.5) / 400)
    series = np.polynomial.chebyshev.Chebyshev.fit(nodes, fun(nodes), degree, domain=[0.0, 0.25])
    return [float(c) for c in series.convert(kind=np.polynomial.Polynomial).coef]


COS = fit(lambda w: np.cos(2 * np.pi * np.sqrt(w)), 8)
SIN = fit(lambda w: np.sin(2 * np.pi * np.sqrt(w)) / np.sqrt(w), 7)
SINPI = fit(lambda w: np.sin(np.pi * np.sqrt(w)) / np.sqrt(w), 6)


def horner(coefs, w):
    value = jnp.full_like(w, coefs[-1])
    for c in coefs[-2::-1]:
        value = value * w + c
    return value


def sin_pi(u):
    u = jnp.minimum(u, 1.0 - u)
    return u * horner(SINPI, u * u)


def kernel(
    off_in, track_in, e_in, sway_in, gain_in, image_ref,
    off_ref, track_ref, e_ref, sway_ref, gain_ref, loaded, halo, et, win, taps, mine, own_b, gath, steer, spin, head, acc, out_a, in_a,
    hs, hr, ms, mr, ss, rs, xs, xr, bs,
):
    r = lax.axis_index("range")
    g = lax.axis_index("ping")
    y = r % 4
    half, q = g // GROUP, g % GROUP
    pos, core = q // 2, q % 2
    base = GROUP * half
    across = (r, g + GROUP - 2 * GROUP * half)
    after = (jnp.minimum(r + 1, NR - 1), g)
    before = (jnp.maximum(r - 1, 0), g)
    crossing = 1 // (y + 1) - 1 // (r + 1) + y // 3 - r // (NR - 1)
    beyond = jnp.clip(r - 1 + 2 * (y // 3), 0, NR - 1)
    far = (beyond, g + GROUP - 2 * GROUP * half)

    pairs = ((track_in, track_ref), (off_in, off_ref), (e_in, e_ref), (sway_in, sway_ref), (gain_in, gain_ref))
    loads = [pltpu.make_async_copy(a, b, loaded.at[i]) for i, (a, b) in enumerate(pairs)]
    barrier = pltpu.get_barrier_semaphore()

    def greet(device):
        pl.semaphore_signal(barrier, 1, device_id=device, device_id_type=MESH)

    @pl.when(crossing == 1)
    def _():
        greet(far)

    greet(across)
    for j in range(1, GROUP):
        greet((r, base + (q + j) % GROUP))

    @pl.when(y > 0)
    def _():
        greet(before)

    @pl.when(y < 3)
    def _():
        greet(after)

    for load in loads:
        load.start()
    for load in loads:
        load.wait()

    lane = lax.broadcasted_iota(jnp.int32, (1, PC), 1)
    centre = lane % C
    for p in range(PD):
        centre = centre + jnp.where(lane // C == p, 2 * track_ref[p], 0)
    mine[g] = centre

    kpos = lax.broadcasted_iota(jnp.int32, (BAND, 1), 0).astype(jnp.float32)
    edge = sin_pi((kpos + 0.5) * (1.0 / BAND))
    edge = edge * edge
    kfull = lax.broadcasted_iota(jnp.int32, (BAND, 128), 0)
    odd = (kfull % 2).astype(jnp.float32)
    for b in range(2):
        sway = jnp.concatenate([sway_ref[4 * b + i : 4 * b + i + 1, :] for i in range(4)], axis=1)
        gain = jnp.concatenate([gain_ref[4 * b + i : 4 * b + i + 1, :] for i in range(4)], axis=1)
        top = sin_pi(sway) * (1.0 / math.pi)
        shift = kfull.astype(jnp.float32) - (BAND / 2 - 1) - sway
        sinc = jnp.where(shift == 0.0, 1.0, (1.0 - 2.0 * odd) * top / jnp.where(shift == 0.0, 1.0, shift))
        taps[b] = sinc * edge * gain

    zeros = jnp.zeros((RD, 128), jnp.float32)

    def lay(block, kind, third):
        for b in range(2):
            et[kind, b, third * RD : (third + 1) * RD, :] = block[b * 128 : (b + 1) * 128, :].astype(jnp.float32).T

    def blank(kind, third):
        for b in range(2):
            et[kind, b, third * RD : (third + 1) * RD, :] = zeros

    quarter = lax.broadcasted_iota(jnp.int32, (BAND + RD, 128), 1) // C

    def align(kind):
        for b in range(2):
            picked = et[kind, b, pl.ds(off_ref[4 * b] + HALO, BAND + RD), :]
            for i in range(1, 4):
                picked = jnp.where(quarter == i, et[kind, b, pl.ds(off_ref[4 * b + i] + HALO, BAND + RD), :], picked)
            win[b] = picked

    def filtered(kind, piece):
        for b in range(2):
            total = [jnp.zeros((8, 128), jnp.float32) for _ in range(PR // 8)]
            for k in range(BAND):
                tap = taps[b, pl.ds(k, 8, stride=0), :]
                for i in range(PR // 8):
                    at = PR * piece + 8 * i + k
                    total[i] = total[i] + tap * win[b, at : at + 8, :]
            block = jnp.concatenate(total, axis=0).astype(jnp.bfloat16)
            rows, lanes = slice(piece * PR, (piece + 1) * PR), slice(b * 128, (b + 1) * 128)
            if kind:
                own_b[rows, lanes] = block
            else:
                gath[0, q, rows, lanes] = block

    lay(e_ref, 0, 1)
    blank(1, 1)

    @pl.when(y == 3)
    def _():
        lay(e_ref, 1, 0)
        blank(1, 2)

    @pl.when(y == 0)
    def _():
        blank(1, 0)
        lay(e_ref, 1, 2)

    @pl.when(crossing == 1)
    def _():
        align(1)
        for piece in range(NC):
            filtered(1, piece)

    pl.semaphore_wait(barrier, GROUP + 2 - 1 // (y + 1) - y // 3 + crossing)

    def halo_copy(way, device):
        return pltpu.make_async_remote_copy(
            e_ref, halo.at[way], hs.at[way], hr.at[way], device_id=device, device_id_type=MESH
        )

    opposite = g + GROUP - 2 * base

    def mine_copy(group, kind, j):
        device = (r, base + (q + j) % GROUP) if j else across
        return pltpu.make_async_remote_copy(
            mine.at[group], mine.at[group], ms.at[kind, j], mr.at[group], device_id=device, device_id_type=MESH
        )

    def far_copy(piece):
        rows = pl.ds(piece * PR, PR)
        return pltpu.make_async_remote_copy(
            own_b.at[rows], gath.at[1, q, rows], bs.at[piece], rs.at[1, q, piece], device_id=far, device_id_type=MESH
        )

    @pl.when(crossing == 1)
    def _():
        for piece in range(NC):
            far_copy(piece).start()
        mine_copy(g, 1, 0).start()

    @pl.when(y < 3)
    def _():
        halo_copy(0, after).start()

    @pl.when(y > 0)
    def _():
        halo_copy(1, before).start()

    for j in range(1, GROUP):
        mine_copy(g, 0, j).start()

    def copy(kind, slot, piece, way):
        rows = pl.ds(piece * PR, PR)
        peer = q + 1 - 2 * core if way == 0 else (q + 2 * way) % GROUP
        return pltpu.make_async_remote_copy(
            gath.at[kind, slot, rows], gath.at[kind, slot, rows], ss.at[kind, slot, piece, way], rs.at[kind, slot, piece],
            device_id=(r, base + peer), device_id_type=MESH,
        )

    def spread(kind, piece):
        for way in (2, 1, 3, 0):
            copy(kind, q, piece, way).start()

    @pl.when(y > 0)
    def _():
        halo_copy(0, after).wait_recv()
        lay(halo.at[0], 0, 0)

    @pl.when(y == 0)
    def _():
        blank(0, 0)

    @pl.when(y < 3)
    def _():
        halo_copy(1, before).wait_recv()
        lay(halo.at[1], 0, 2)

    @pl.when(y == 3)
    def _():
        blank(0, 2)

    align(0)
    for piece in range(NC):
        filtered(0, piece)
        spread(0, piece)

    @pl.when(crossing == 1)
    def _():
        mine_copy(opposite, 1, 0).wait_recv()
        for j in range(1, GROUP):
            mine_copy(opposite, 1, j).start()

    scale = 1.0 / math.sqrt(NP * PC)

    def group_of(kind, slot):
        return slot + base + kind * (GROUP - 2 * base)

    full = (64 * 2 * (2 * r + 65)).astype(jnp.float32)

    def wave(squares, factor):
        turn = 1.0 / jnp.full(squares.shape, full, jnp.float32)
        u = (squares - jnp.floor(squares * turn + 0.5) * full) * turn
        w = u * u
        weight = jnp.exp(squares * (-1.0 / (8.0 * 65536.0))) * factor
        return weight * horner(COS, w), weight * (u * horner(SIN, w))

    eight = lax.broadcasted_iota(jnp.int32, (128, 128), 0)
    spin[0], spin[1] = wave((64 * (eight // 8) * (eight % 8)).astype(jnp.float32), 1.0)

    def build(kind, slot):
        centres = mine[group_of(kind, slot)]
        starts = [2 * ROWS * g - centres, 2 * ROWS * opposite - centres]
        step = lax.broadcasted_iota(jnp.int32, (16, PC), 0)
        n = jnp.concatenate([16 * step + start for start in starts], axis=0).astype(jnp.float32)
        head[0], head[1] = wave(n * n, scale)
        s8 = lax.broadcasted_iota(jnp.int32, (8, PC), 0)
        turned = jnp.concatenate([4 * s8 * (start + s8) for start in starts], axis=0).astype(jnp.float32)
        cos, sin = wave(turned, 1.0)
        for part in range(2):
            cos8, sin8 = cos[8 * part : 8 * part + 8], sin[8 * part : 8 * part + 8]

            for i in range(ROWS // 16):
                real, imag = [], []
                for j in range(2):
                    at = 16 * i + 8 * j
                    cr = jnp.concatenate([spin[0, at : at + 8, :]] * 2, axis=1)
                    ci = jnp.concatenate([spin[1, at : at + 8, :]] * 2, axis=1)
                    br, bi = cos8 * cr - sin8 * ci, cos8 * ci + sin8 * cr
                    hr = head[0, pl.ds(16 * part + 2 * i + j, 8, stride=0), :]
                    hi = head[1, pl.ds(16 * part + 2 * i + j, 8, stride=0), :]
                    real.append(hr * br - hi * bi)
                    imag.append(hr * bi + hi * br)
                at = 2 * ROWS * part + 16 * i
                steer[kind, slot, at : at + 16, :] = jnp.concatenate(real, axis=0).astype(jnp.bfloat16)
                at = at + ROWS
                steer[kind, slot, at : at + 16, :] = jnp.concatenate(imag, axis=0).astype(jnp.bfloat16)

    def build_all(kind):
        for i, slot in enumerate(order):
            if i:
                mine_copy(group_of(kind, slot), 0, 1).wait_recv()

        def one(slot, carry):
            build(kind, slot)
            return carry

        lax.fori_loop(0, GROUP, one, 0)

    def slots(way):
        return (q + 2 * way) % GROUP

    twin = q + 1 - 2 * core
    order = [q, twin] + [s for way in (1, 3, 2) for s in (slots(way), (twin + 2 * way) % GROUP)]

    build_all(0)

    def add(part, kind, slot, first=False):
        product = lax.dot_general(
            gath[kind, slot], steer[kind, slot, 2 * ROWS * part : 2 * ROWS * (part + 1), :],
            (((1,), (1,)), ((), ())), preferred_element_type=jnp.float32,
        )
        acc[part] = product if first else acc[part] + product

    def arrive(kind, piece):
        for way in (1, 3, 2):
            copy(kind, slots(way), piece, 0).wait_recv()
            copy(kind, slots(way), piece, 0).start()

    def outer(kind):
        for way in (0, 1, 3, 2):
            add(1, kind, slots(way), kind == 0 and way == 0)
        for way in (0, 1, 3, 2):
            slot = (twin + 2 * way) % GROUP
            for piece in range(NC):
                copy(kind, slot, piece, 0).wait_recv()
            add(1, kind, slot)

    def inner(kind):
        for i, slot in enumerate(order):
            add(0, kind, slot, kind == 0 and i == 0)

    across_copy = pltpu.make_async_remote_copy(
        out_a, in_a, xs.at[0], xr.at[0], device_id=across, device_id_type=MESH
    )

    def cross():
        out_a[...] = acc[1].astype(jnp.bfloat16)
        across_copy.start()

    for piece in range(NC):
        arrive(0, piece)

    @pl.when(crossing == 1)
    def _():
        for piece in range(NC):
            copy(1, q, piece, 0).wait_recv()
            spread(1, piece)
        build_all(1)

    outer(0)

    @pl.when(crossing == 0)
    def _():
        cross()

    inner(0)

    @pl.when(crossing == 1)
    def _():
        for piece in range(NC):
            arrive(1, piece)
        outer(1)
        cross()
        inner(1)

    @pl.when(y < 3)
    def _():
        halo_copy(0, after).wait_send()

    @pl.when(y > 0)
    def _():
        halo_copy(1, before).wait_send()

    for j in range(1, GROUP):
        mine_copy(g, 0, j).wait_send()

    def left(kind):
        for piece in range(NC):
            for way in range(4):
                copy(kind, q, piece, way).wait_send()
                if way:
                    copy(kind, slots(way), piece, 0).wait_send()

    left(0)

    @pl.when(crossing == 1)
    def _():
        left(1)
        for piece in range(NC):
            far_copy(piece).wait_send()
        mine_copy(g, 1, 0).wait_send()
        for j in range(1, GROUP):
            mine_copy(opposite, 1, j).wait_send()

    across_copy.wait_recv()
    acc[0] = acc[0] + in_a[...].astype(jnp.float32)

    image_ref[0] = acc[0, :, 0:ROWS].T
    image_ref[1] = acc[0, :, ROWS : 2 * ROWS].T
    across_copy.wait_send()


def shards(echoes, band_offset, sway_delay, channel_gain, track_bin):
    whole = pl.BlockSpec(memory_space=pltpu.VMEM)
    kept = pl.BlockSpec(memory_space=pltpu.HBM)
    out = jax.ShapeDtypeStruct((2, ROWS, RD), jnp.float32)
    dma = pltpu.SemaphoreType.DMA
    image = pl.pallas_call(
        kernel,
        out_shape=out,
        in_specs=[kept] * 5,
        out_specs=whole,
        scratch_shapes=[
            pltpu.SMEM((PD,), jnp.int32),
            pltpu.SMEM((PD,), jnp.int32),
            pltpu.VMEM((PC, RD), jnp.bfloat16),
            pltpu.VMEM((PD, C), jnp.float32),
            pltpu.VMEM((PD, C), jnp.float32),
            dma((5,)),
            pltpu.VMEM((2, PC, RD), jnp.bfloat16),
            pltpu.VMEM((2, 2, 3 * RD, 128), jnp.float32),
            pltpu.VMEM((2, BAND + RD, 128), jnp.float32),
            pltpu.VMEM((2, BAND, 128), jnp.float32),
            pltpu.VMEM((NP, 1, PC), jnp.int32),
            pltpu.VMEM((RD, PC), jnp.bfloat16),
            pltpu.VMEM((2, GROUP, RD, PC), jnp.bfloat16),
            pltpu.VMEM((2, GROUP, 4 * ROWS, PC), jnp.bfloat16),
            pltpu.VMEM((2, 128, 128), jnp.float32),
            pltpu.VMEM((2, 32, PC), jnp.float32),
            pltpu.VMEM((2, RD, 2 * ROWS), jnp.float32),
            pltpu.VMEM((RD, 2 * ROWS), jnp.bfloat16),
            pltpu.VMEM((RD, 2 * ROWS), jnp.bfloat16),
            dma((2,)),
            dma((2,)),
            dma((2, GROUP)),
            dma((NP,)),
            dma((2, GROUP, NC, 4)),
            dma((2, GROUP, NC)),
            dma((1,)),
            dma((1,)),
            dma((NC,)),
        ],
        compiler_params=pltpu.CompilerParams(collective_id=0, has_side_effects=True),
    )(band_offset, track_bin, echoes.reshape(PC, RD), sway_delay, channel_gain)
    return (image[0], image[1])


def solution(mesh):
    return jax.shard_map(
        shards,
        mesh=mesh,
        in_specs=(P("ping", None, "range"), P("ping"), P("ping", None), P("ping", None), P("ping")),
        out_specs=(P("ping", "range"), P("ping", "range")),
        check_vma=False,
    )
```

```python
import functools
import math

import jax
import jax.numpy as jnp
import numpy as np
from jax import lax
from jax.experimental import pallas as pl
from jax.experimental.pallas import tpu as pltpu
from jax.sharding import PartitionSpec as P

X = 2048
BAND = 64
HALO = 128
NR = 32
NP = 16
PD = 8
C = 32
RD = 128
PC = PD * C
ROWS = X // NP
GROUP = 8
NC = 1
PR = RD // NC
MESH = pl.DeviceIdType.MESH


def fit(fun, degree):
    nodes = 0.125 + 0.125 * np.cos(np.pi * (np.arange(400) + 0.5) / 400)
    series = np.polynomial.chebyshev.Chebyshev.fit(nodes, fun(nodes), degree, domain=[0.0, 0.25])
    return [float(c) for c in series.convert(kind=np.polynomial.Polynomial).coef]


COS = fit(lambda w: np.cos(2 * np.pi * np.sqrt(w)), 8)
SIN = fit(lambda w: np.sin(2 * np.pi * np.sqrt(w)) / np.sqrt(w), 7)
SINPI = fit(lambda w: np.sin(np.pi * np.sqrt(w)) / np.sqrt(w), 6)


def horner(coefs, w):
    value = jnp.full_like(w, coefs[-1])
    for c in coefs[-2::-1]:
        value = value * w + c
    return value


def sin_pi(u):
    u = jnp.minimum(u, 1.0 - u)
    return u * horner(SINPI, u * u)


def kernel(
    off_in, track_in, e_in, sway_in, gain_in, image_ref,
    off_ref, track_ref, e_ref, sway_ref, gain_ref, loaded, halo, et, win, taps, mine, own_b, gath, steer, spin, head, acc, out_a, in_a,
    hs, hr, ms, mr, ss, rs, xs, xr, bs,
):
    r = lax.axis_index("range")
    g = lax.axis_index("ping")
    y = r % 4
    half, q = g // GROUP, g % GROUP
    pos, core = q // 2, q % 2
    base = GROUP * half
    across = (r, g + GROUP - 2 * GROUP * half)
    after = (jnp.minimum(r + 1, NR - 1), g)
    before = (jnp.maximum(r - 1, 0), g)
    crossing = 1 // (y + 1) - 1 // (r + 1) + y // 3 - r // (NR - 1)
    beyond = jnp.clip(r - 1 + 2 * (y // 3), 0, NR - 1)
    far = (beyond, g + GROUP - 2 * GROUP * half)

    pairs = ((track_in, track_ref), (off_in, off_ref), (e_in, e_ref), (sway_in, sway_ref), (gain_in, gain_ref))
    loads = [pltpu.make_async_copy(a, b, loaded.at[i]) for i, (a, b) in enumerate(pairs)]
    barrier = pltpu.get_barrier_semaphore()

    def greet(device):
        pl.semaphore_signal(barrier, 1, device_id=device, device_id_type=MESH)

    @pl.when(crossing == 1)
    def _():
        greet(far)

    greet(across)
    for j in range(1, GROUP):
        greet((r, base + (q + j) % GROUP))

    @pl.when(y > 0)
    def _():
        greet(before)

    @pl.when(y < 3)
    def _():
        greet(after)

    for load in loads:
        load.start()
    for load in loads:
        load.wait()

    lane = lax.broadcasted_iota(jnp.int32, (1, PC), 1)
    centre = lane % C
    for p in range(PD):
        centre = centre + jnp.where(lane // C == p, 2 * track_ref[p], 0)
    mine[g] = centre

    kpos = lax.broadcasted_iota(jnp.int32, (BAND, 1), 0).astype(jnp.float32)
    edge = sin_pi((kpos + 0.5) * (1.0 / BAND))
    edge = edge * edge
    kfull = lax.broadcasted_iota(jnp.int32, (BAND, 128), 0)
    odd = (kfull % 2).astype(jnp.float32)
    for b in range(2):
        sway = jnp.concatenate([sway_ref[4 * b + i : 4 * b + i + 1, :] for i in range(4)], axis=1)
        gain = jnp.concatenate([gain_ref[4 * b + i : 4 * b + i + 1, :] for i in range(4)], axis=1)
        top = sin_pi(sway) * (1.0 / math.pi)
        shift = kfull.astype(jnp.float32) - (BAND / 2 - 1) - sway
        sinc = jnp.where(shift == 0.0, 1.0, (1.0 - 2.0 * odd) * top / jnp.where(shift == 0.0, 1.0, shift))
        taps[b] = sinc * edge * gain

    zeros = jnp.zeros((RD, 128), jnp.float32)

    def lay(block, kind, third):
        for b in range(2):
            et[kind, b, third * RD : (third + 1) * RD, :] = block[b * 128 : (b + 1) * 128, :].astype(jnp.float32).T

    def blank(kind, third):
        for b in range(2):
            et[kind, b, third * RD : (third + 1) * RD, :] = zeros

    quarter = lax.broadcasted_iota(jnp.int32, (BAND + RD, 128), 1) // C

    def align(kind):
        for b in range(2):
            picked = et[kind, b, pl.ds(off_ref[4 * b] + HALO, BAND + RD), :]
            for i in range(1, 4):
                picked = jnp.where(quarter == i, et[kind, b, pl.ds(off_ref[4 * b + i] + HALO, BAND + RD), :], picked)
            win[b] = picked

    def filtered(kind, piece):
        for b in range(2):
            total = [jnp.zeros((8, 128), jnp.float32) for _ in range(PR // 8)]
            for k in range(BAND):
                tap = taps[b, pl.ds(k, 8, stride=0), :]
                for i in range(PR // 8):
                    at = PR * piece + 8 * i + k
                    total[i] = total[i] + tap * win[b, at : at + 8, :]
            block = jnp.concatenate(total, axis=0).astype(jnp.bfloat16)
            rows, lanes = slice(piece * PR, (piece + 1) * PR), slice(b * 128, (b + 1) * 128)
            if kind:
                own_b[rows, lanes] = block
            else:
                gath[0, q, rows, lanes] = block

    lay(e_ref, 0, 1)
    blank(1, 1)

    @pl.when(y == 3)
    def _():
        lay(e_ref, 1, 0)
        blank(1, 2)

    @pl.when(y == 0)
    def _():
        blank(1, 0)
        lay(e_ref, 1, 2)

    @pl.when(crossing == 1)
    def _():
        align(1)
        for piece in range(NC):
            filtered(1, piece)

    pl.semaphore_wait(barrier, GROUP + 2 - 1 // (y + 1) - y // 3 + crossing)

    def halo_copy(way, device):
        return pltpu.make_async_remote_copy(
            e_ref, halo.at[way], hs.at[way], hr.at[way], device_id=device, device_id_type=MESH
        )

    opposite = g + GROUP - 2 * base

    def mine_copy(group, kind, j):
        device = (r, base + (q + j) % GROUP) if j else across
        return pltpu.make_async_remote_copy(
            mine.at[group], mine.at[group], ms.at[kind, j], mr.at[group], device_id=device, device_id_type=MESH
        )

    def far_copy(piece):
        rows = pl.ds(piece * PR, PR)
        return pltpu.make_async_remote_copy(
            own_b.at[rows], gath.at[1, q, rows], bs.at[piece], rs.at[1, q, piece], device_id=far, device_id_type=MESH
        )

    @pl.when(crossing == 1)
    def _():
        for piece in range(NC):
            far_copy(piece).start()
        mine_copy(g, 1, 0).start()

    @pl.when(y < 3)
    def _():
        halo_copy(0, after).start()

    @pl.when(y > 0)
    def _():
        halo_copy(1, before).start()

    for j in range(1, GROUP):
        mine_copy(g, 0, j).start()

    def copy(kind, slot, piece, way):
        rows = pl.ds(piece * PR, PR)
        peer = q + 1 - 2 * core if way == 0 else (q + 2 * way) % GROUP
        return pltpu.make_async_remote_copy(
            gath.at[kind, slot, rows], gath.at[kind, slot, rows], ss.at[kind, slot, piece, way], rs.at[kind, slot, piece],
            device_id=(r, base + peer), device_id_type=MESH,
        )

    def spread(kind, piece):
        for way in (2, 1, 3, 0):
            copy(kind, q, piece, way).start()

    @pl.when(y > 0)
    def _():
        halo_copy(0, after).wait_recv()
        lay(halo.at[0], 0, 0)

    @pl.when(y == 0)
    def _():
        blank(0, 0)

    @pl.when(y < 3)
    def _():
        halo_copy(1, before).wait_recv()
        lay(halo.at[1], 0, 2)

    @pl.when(y == 3)
    def _():
        blank(0, 2)

    align(0)
    for piece in range(NC):
        filtered(0, piece)
        spread(0, piece)

    @pl.when(crossing == 1)
    def _():
        mine_copy(opposite, 1, 0).wait_recv()
        for j in range(1, GROUP):
            mine_copy(opposite, 1, j).start()

    scale = 1.0 / math.sqrt(NP * PC)

    def group_of(kind, slot):
        return slot + base + kind * (GROUP - 2 * base)

    full = (64 * 2 * (2 * r + 65)).astype(jnp.float32)

    def wave(squares, factor):
        turn = 1.0 / jnp.full(squares.shape, full, jnp.float32)
        u = (squares - jnp.floor(squares * turn + 0.5) * full) * turn
        w = u * u
        weight = jnp.exp(squares * (-1.0 / (8.0 * 65536.0))) * factor
        return weight * horner(COS, w), weight * (u * horner(SIN, w))

    eight = lax.broadcasted_iota(jnp.int32, (128, 128), 0)
    spin[0], spin[1] = wave((64 * (eight // 8) * (eight % 8)).astype(jnp.float32), 1.0)

    def build(kind, slot):
        centres = mine[group_of(kind, slot)]
        starts = [2 * ROWS * g - centres, 2 * ROWS * opposite - centres]
        step = lax.broadcasted_iota(jnp.int32, (16, PC), 0)
        n = jnp.concatenate([16 * step + start for start in starts], axis=0).astype(jnp.float32)
        head[0], head[1] = wave(n * n, scale)
        s8 = lax.broadcasted_iota(jnp.int32, (8, PC), 0)
        turned = jnp.concatenate([4 * s8 * (start + s8) for start in starts], axis=0).astype(jnp.float32)
        cos, sin = wave(turned, 1.0)
        for part in range(2):
            cos8, sin8 = cos[8 * part : 8 * part + 8], sin[8 * part : 8 * part + 8]

            for i in range(ROWS // 16):
                real, imag = [], []
                for j in range(2):
                    at = 16 * i + 8 * j
                    cr = jnp.concatenate([spin[0, at : at + 8, :]] * 2, axis=1)
                    ci = jnp.concatenate([spin[1, at : at + 8, :]] * 2, axis=1)
                    br, bi = cos8 * cr - sin8 * ci, cos8 * ci + sin8 * cr
                    hr = head[0, pl.ds(16 * part + 2 * i + j, 8, stride=0), :]
                    hi = head[1, pl.ds(16 * part + 2 * i + j, 8, stride=0), :]
                    real.append(hr * br - hi * bi)
                    imag.append(hr * bi + hi * br)
                at = 2 * ROWS * part + 16 * i
                steer[kind, slot, at : at + 16, :] = jnp.concatenate(real, axis=0).astype(jnp.bfloat16)
                at = at + ROWS
                steer[kind, slot, at : at + 16, :] = jnp.concatenate(imag, axis=0).astype(jnp.bfloat16)

    def build_all(kind):
        for i, slot in enumerate(order):
            if i:
                mine_copy(group_of(kind, slot), 0, 1).wait_recv()

        def one(slot, carry):
            build(kind, slot)
            return carry

        lax.fori_loop(0, GROUP, one, 0)

    def slots(way):
        return (q + 2 * way) % GROUP

    twin = q + 1 - 2 * core
    order = [q, twin] + [s for way in (1, 3, 2) for s in (slots(way), (twin + 2 * way) % GROUP)]

    build_all(0)

    def add(part, kind, slot, first=False):
        product = lax.dot_general(
            gath[kind, slot], steer[kind, slot, 2 * ROWS * part : 2 * ROWS * (part + 1), :],
            (((1,), (1,)), ((), ())), preferred_element_type=jnp.float32,
        )
        acc[part] = product if first else acc[part] + product

    def arrive(kind, piece):
        for way in (1, 3, 2):
            copy(kind, slots(way), piece, 0).wait_recv()
            copy(kind, slots(way), piece, 0).start()

    def outer(kind):
        for way in (0, 1, 3, 2):
            add(1, kind, slots(way), kind == 0 and way == 0)
        for way in (0, 1, 3, 2):
            slot = (twin + 2 * way) % GROUP
            for piece in range(NC):
                copy(kind, slot, piece, 0).wait_recv()
            add(1, kind, slot)

    def inner(kind):
        for i, slot in enumerate(order):
            add(0, kind, slot, kind == 0 and i == 0)

    across_copy = pltpu.make_async_remote_copy(
        out_a, in_a, xs.at[0], xr.at[0], device_id=across, device_id_type=MESH
    )

    def cross():
        out_a[...] = acc[1].astype(jnp.bfloat16)
        across_copy.start()

    @pl.when(crossing == 1)
    def _():
        for piece in range(NC):
            copy(1, q, piece, 0).wait_recv()
            spread(1, piece)

    for piece in range(NC):
        arrive(0, piece)

    @pl.when(crossing == 1)
    def _():
        build_all(1)

    outer(0)

    @pl.when(crossing == 0)
    def _():
        cross()

    inner(0)

    @pl.when(crossing == 1)
    def _():
        for piece in range(NC):
            arrive(1, piece)
        outer(1)
        cross()
        inner(1)

    @pl.when(y < 3)
    def _():
        halo_copy(0, after).wait_send()

    @pl.when(y > 0)
    def _():
        halo_copy(1, before).wait_send()

    for j in range(1, GROUP):
        mine_copy(g, 0, j).wait_send()

    def left(kind):
        for piece in range(NC):
            for way in range(4):
                copy(kind, q, piece, way).wait_send()
                if way:
                    copy(kind, slots(way), piece, 0).wait_send()

    left(0)

    @pl.when(crossing == 1)
    def _():
        left(1)
        for piece in range(NC):
            far_copy(piece).wait_send()
        mine_copy(g, 1, 0).wait_send()
        for j in range(1, GROUP):
            mine_copy(opposite, 1, j).wait_send()

    across_copy.wait_recv()
    acc[0] = acc[0] + in_a[...].astype(jnp.float32)

    image_ref[0] = acc[0, :, 0:ROWS].T
    image_ref[1] = acc[0, :, ROWS : 2 * ROWS].T
    across_copy.wait_send()


def shards(echoes, band_offset, sway_delay, channel_gain, track_bin):
    whole = pl.BlockSpec(memory_space=pltpu.VMEM)
    kept = pl.BlockSpec(memory_space=pltpu.HBM)
    out = jax.ShapeDtypeStruct((2, ROWS, RD), jnp.float32)
    dma = pltpu.SemaphoreType.DMA
    image = pl.pallas_call(
        kernel,
        out_shape=out,
        in_specs=[kept] * 5,
        out_specs=whole,
        scratch_shapes=[
            pltpu.SMEM((PD,), jnp.int32),
            pltpu.SMEM((PD,), jnp.int32),
            pltpu.VMEM((PC, RD), jnp.bfloat16),
            pltpu.VMEM((PD, C), jnp.float32),
            pltpu.VMEM((PD, C), jnp.float32),
            dma((5,)),
            pltpu.VMEM((2, PC, RD), jnp.bfloat16),
            pltpu.VMEM((2, 2, 3 * RD, 128), jnp.float32),
            pltpu.VMEM((2, BAND + RD, 128), jnp.float32),
            pltpu.VMEM((2, BAND, 128), jnp.float32),
            pltpu.VMEM((NP, 1, PC), jnp.int32),
            pltpu.VMEM((RD, PC), jnp.bfloat16),
            pltpu.VMEM((2, GROUP, RD, PC), jnp.bfloat16),
            pltpu.VMEM((2, GROUP, 4 * ROWS, PC), jnp.bfloat16),
            pltpu.VMEM((2, 128, 128), jnp.float32),
            pltpu.VMEM((2, 32, PC), jnp.float32),
            pltpu.VMEM((2, RD, 2 * ROWS), jnp.float32),
            pltpu.VMEM((RD, 2 * ROWS), jnp.bfloat16),
            pltpu.VMEM((RD, 2 * ROWS), jnp.bfloat16),
            dma((2,)),
            dma((2,)),
            dma((2, GROUP)),
            dma((NP,)),
            dma((2, GROUP, NC, 4)),
            dma((2, GROUP, NC)),
            dma((1,)),
            dma((1,)),
            dma((NC,)),
        ],
        compiler_params=pltpu.CompilerParams(collective_id=0, has_side_effects=True),
    )(band_offset, track_bin, echoes.reshape(PC, RD), sway_delay, channel_gain)
    return (image[0], image[1])


def solution(mesh):
    return jax.shard_map(
        shards,
        mesh=mesh,
        in_specs=(P("ping", None, "range"), P("ping"), P("ping", None), P("ping", None), P("ping")),
        out_specs=(P("ping", "range"), P("ping", "range")),
        check_vma=False,
    )
```
